32 devices in a mesh: grp: 4 (over y, x), tile: 8 (over z, core).
Axes of the slice: x: 2, y: 2, z: 4, core: 2. Of those that a mesh axis runs over, the one named last changes fastest.
Arguments:
- temp: bfloat16 [48, 64, 2048], P(None, 'grp', 'tile'), may hold values from -6 to 6
- humid: bfloat16 [48, 64, 2048], P(None, 'grp', 'tile'), may hold values from -5 to 5
- parent: int32 [64, 2048], P('grp', 'tile'), may hold values from 0 to 8191, as said below
- kabs: float32 [112, 48], replicated, may hold values from 0.003 to 1
- planck: float32 [112], replicated, may hold values from 0.5 to 2
- top_flux: float32 [112], replicated, may hold values from 0 to 2
Outputs:
- temp_next: bfloat16 [48, 64, 2048], P(None, 'grp', 'tile')
The draws below stay inside these ranges and needn't reach their ends.
Inputs may be any that keep to these rules, and one draw needn't show every extreme that they name: parent // 1024 is the tile index, in the same region, of the device owning that parent column; the fine cells of one device name any one owner at most 1024 times.
All inputs are finite; a program needn't handle non-finite values.
Results may differ from the reference program's by a relative error of at most 0.005.
Values may be sent and summed in bfloat16 or wider, within the bound.
A program may use at most 64 MiB of HBM per device.

```python
import math
import jax
import jax.numpy as jnp
from jax import lax

NLEV = 48
G = 112
FR = 16
FCOL = 256
CC = 1024
NCO = 8192
NY = 64
NX = 2048
N_GRP = 4
N_TILE = 8


def draw_parent(key, part):
    fine = FR * FCOL
    assigned_slots = 2 * fine
    capacity_limit = assigned_slots // N_TILE
    owned = fine // 4
    keys = jax.random.split(jax.random.fold_in(key, 17), 4)
    rank_keys = jax.random.split(keys[0], N_GRP)
    hot_rank = jax.vmap(lambda k: jax.random.permutation(k, N_TILE))(rank_keys)
    busiest_flag = (hot_rank < max(N_TILE // 4, 1)).astype(jnp.int32)
    random_jitter = jax.random.randint(keys[1], (N_GRP, N_TILE, assigned_slots), 0, 512)
    slot_numbers = jnp.arange(assigned_slots, dtype=jnp.int32)
    extra_priority = busiest_flag[:, slot_numbers // capacity_limit]
    ranking_score = (random_jitter + 512 * extra_priority[:, None, :]) * assigned_slots + slot_numbers[None, None, :]
    unused, chosen = lax.top_k(ranking_score, fine)
    chosen = jax.random.permutation(keys[2], chosen, axis=2, independent=True)
    owner = chosen // capacity_limit
    local = jax.random.randint(keys[3], (N_GRP, N_TILE, fine), 0, owned)
    parent = (owner * owned + local).astype(jnp.int32)
    parent = parent.reshape(N_GRP, N_TILE, FR, FCOL)
    return jnp.transpose(parent, (0, 2, 1, 3)).reshape(N_GRP * FR, N_TILE * FCOL)


def block_levels(own_key, shape, cuts, smallest, high):
    loudness = 1.0
    for dim, shards_of in cuts:
        heights = jax.random.uniform(jax.random.fold_in(jax.random.fold_in(own_key, 6), dim), (shards_of,), jnp.float32, smallest / len(cuts), high / len(cuts))
        loudness = loudness * jnp.repeat(jnp.exp(heights), shape[dim] // shards_of).reshape((-1,) + (1,) * (len(shape) - 1 - dim))
    return loudness


def gaussian(key, extent, width, limit, cuts=(), kind=jnp.bfloat16):
    drawn = width * jax.random.normal(key, extent, jnp.float32)
    if cuts:
        drawn = drawn * block_levels(key, extent, cuts, -0.22, 0.18)
    return jnp.clip(drawn, -limit, limit).astype(kind)


def setup_inputs(seed: int = 0) -> dict:
    seeds = jax.random.split(jax.random.key(seed), 7)
    return {
        "temp": gaussian(seeds[0], (NLEV, NY, NX), 1.0, 6.0, ((1, 4), (2, 8))),
        "humid": gaussian(seeds[1], (NLEV, NY, NX), 1.0, 5.0, ((1, 4), (2, 8))),
        "parent": draw_parent(jax.random.fold_in(seeds[6], 71), 0),
        "kabs": jnp.clip(jnp.exp(jax.random.uniform(seeds[3], (G, NLEV), jnp.float32, math.log(0.003), math.log(1.0))), 0.003, 1.0),
        "planck": jnp.clip(jnp.exp(jax.random.uniform(seeds[4], (G,), jnp.float32, math.log(0.5), math.log(2.0))), 0.5, 2.0),
        "top_flux": jnp.clip(jax.random.uniform(seeds[5], (G,), jnp.float32, 0.0, 2.0), 0.0, 2.0),
    }


def recur(coef, source, init):
    levels = coef.shape[0]
    blocks = levels // 8
    rest = coef.shape[1:]
    coef4 = coef.reshape((blocks, 8) + rest)
    source4 = source.reshape((blocks, 8) + rest)
    prod_list = []
    part_list = []
    prod_now = jnp.ones((blocks,) + rest, jnp.float32)
    part_now = jnp.zeros((blocks,) + rest, jnp.float32)
    for inner in range(8):
        prod_now = coef4[:, inner] * prod_now
        part_now = coef4[:, inner] * part_now + source4[:, inner]
        prod_list.append(prod_now)
        part_list.append(part_now)
    starts = []
    carry = init
    for outer in range(blocks):
        starts.append(carry)
        carry = prod_list[7][outer] * carry + part_list[7][outer]
    start = jnp.stack(starts, 0)
    result = jnp.stack([prod_list[j] * start + part_list[j] for j in range(8)], 1)
    return result.reshape((levels,) + rest)


def radiate(tc, hc, kabs, planck, top_flux):
    levels, count = tc.shape
    kblk = kabs.reshape(-1, 16, levels)
    pblk = planck.reshape(-1, 16)
    tblk = top_flux.reshape(-1, 16)
    absorb = jnp.exp(0.5 * hc)[:, None, :]
    emit = jnp.exp(0.25 * tc)[:, None, :]

    def one_block(items):
        k_blk, p_blk, t_blk = items
        tau = jnp.transpose(k_blk)[:, :, None] * absorb
        trans = jnp.exp(-tau)
        source = p_blk[None, :, None] * emit * (1.0 - trans)
        top = jnp.broadcast_to(t_blk[:, None], (16, count)).astype(jnp.float32)
        down = recur(trans, source, top)
        up = recur(trans[::-1], source[::-1], 0.3 * down[-1])[::-1]
        net = down - up
        top_net = top - up[0]
        before = jnp.concatenate([top_net[None], net[:-1]], 0)
        return jnp.sum(before - net, axis=1)

    parts = lax.map(one_block, (kblk, pblk, tblk))
    return jnp.sum(parts, axis=0) * (levels / kabs.shape[0])


def laplace(field):
    value = field.astype(jnp.float32)
    return (jnp.roll(value, 1, 1) + jnp.roll(value, -1, 1) + jnp.roll(value, 1, 2) + jnp.roll(value, -1, 2) - 4.0 * value)


def reference(temp, humid, parent, kabs, planck, top_flux):
    levels = temp.shape[0]
    first = (temp.astype(jnp.float32) + 0.2 * laplace(temp)).astype(jnp.bfloat16)
    region = (jnp.arange(NY) // FR).astype(jnp.int32)
    global_id = (region[:, None] * NCO + parent).reshape(-1)
    total = N_GRP * NCO
    values = jnp.concatenate([temp.reshape(levels, -1), humid.reshape(levels, -1)], 0).astype(jnp.float32)
    sums = jax.ops.segment_sum(jnp.transpose(values), global_id, num_segments=total)
    counts = jax.ops.segment_sum(jnp.ones(global_id.shape, jnp.float32), global_id, num_segments=total)
    means = sums / jnp.maximum(counts, 1.0)[:, None]
    blocks = means.reshape(total // CC, CC, 2 * levels)

    def per_owner(block):
        tc = jnp.transpose(block[:, :levels])
        hc = jnp.transpose(block[:, levels:])
        return radiate(tc, hc, kabs, planck, top_flux)

    heat = lax.map(per_owner, blocks)
    heat_c = jnp.transpose(heat, (1, 0, 2)).reshape(levels, total).astype(jnp.bfloat16)
    hmean = jnp.transpose(means[:, levels:]).astype(jnp.bfloat16)
    heat_f = heat_c[:, global_id].astype(jnp.float32) + 0.5 * (humid.reshape(levels, -1).astype(jnp.float32) - hmean[:, global_id].astype(jnp.float32))
    second = (first.astype(jnp.float32) + 0.5 * heat_f.reshape(temp.shape)).astype(jnp.bfloat16)
    return (second.astype(jnp.float32) + 0.2 * laplace(second)).astype(jnp.bfloat16)
```

```python
import functools
import math

import jax
import jax.numpy as jnp
from jax import lax
from jax.experimental import pallas as pl
from jax.experimental.pallas import tpu as pltpu
from jax.sharding import PartitionSpec as P

F32 = jnp.float32
BF16 = jnp.bfloat16
VMEM_LIMIT = 60 * 1024 * 1024
VSPEC = pl.BlockSpec(memory_space=pltpu.VMEM)


def partial_kernel(chunks, vals_ref, parent_ref, out_ref, onehot, masked):
    rows, feats, lanes = vals_ref.shape
    owner = pl.program_id(0)

    @pl.when(owner == 0)
    def _():
        lo_iota = lax.broadcasted_iota(jnp.int32, (lanes, lanes), 0)
        for r in range(rows):
            low = parent_ref[r : r + 1, :] % lanes
            onehot[:, r * lanes : (r + 1) * lanes] = (lo_iota == low).astype(F32).astype(BF16)

    for r in range(rows):
        high = jnp.broadcast_to(parent_ref[r : r + 1, :] // lanes, (16, lanes))
        for c in range(chunks):
            mask = (high == owner * chunks + c).astype(F32).astype(BF16)
            for v in range(feats // 16):
                at = c * feats + v * 16
                masked[at : at + 16, r * lanes : (r + 1) * lanes] = (
                    vals_ref[r, v * 16 : (v + 1) * 16, :] * mask
                )
    total = lax.dot_general(
        masked[...], onehot[...], (((1,), (1,)), ((), ())), preferred_element_type=F32
    )
    out_ref[0] = total.astype(BF16)
    for c in range(chunks):
        at = slice((c + 1) * feats - 16, (c + 1) * feats)
        count = total[at]
        high = jnp.floor(count * (1.0 / 32.0))
        row = lax.broadcasted_iota(jnp.int32, count.shape, 0)
        out_ref[0, at, :] = jnp.where(row == 0, high, count - 32.0 * high).astype(BF16)


def radiate_kernel(levels, feats, recv_ref, kabs_ref, planck_ref, top_ref, out_ref, sums, absorb, emit, trans, net, heat):
    tiles = recv_ref.shape[0]
    lanes = recv_ref.shape[2]
    chunks = recv_ref.shape[1] // feats
    octets = kabs_ref.shape[1] // 8
    group = octets // 2 if octets % 2 == 0 else octets
    width = 128

    def add(i, carry):
        at = pl.ds(pl.multiple_of(i * 16, 16), 16)
        acc = recv_ref[0, at, :].astype(F32)
        for s in range(1, tiles):
            acc = acc + recv_ref[s, at, :].astype(F32)
        sums[at, :] = acc
        return carry

    lax.fori_loop(0, chunks * feats // 16, add, 0)
    for c in range(chunks):
        base = c * feats
        cnt = sums[base + 2 * levels : base + 2 * levels + 1, :] * 32.0
        cnt = cnt + sums[base + 2 * levels + 1 : base + 2 * levels + 2, :]
        cnt = jnp.maximum(cnt, 1.0)
        for j in range(lanes // width):
            part = slice(j * width, (j + 1) * width)
            ct = c * (lanes // width) + j
            tc = sums[base : base + levels, part] / cnt[:, part]
            hc = sums[base + levels : base + 2 * levels, part] / cnt[:, part]
            emit[ct] = jnp.exp(0.25 * tc)
            absorb[ct] = jnp.exp(0.5 * hc) * (-math.log2(math.e))
            heat[ct] = -0.5 * hc

    scale = levels / (octets * 8)

    def column(ct, carry):
        for half in range(octets // group):
            gs = [(half * group + p) * 8 for p in range(group)]
            planck = [planck_ref[g : g + 8, :] for g in gs]
            down = [top_ref[g : g + 8, :] for g in gs]
            if half == 0:
                before = sum(down[1:], down[0])
                net[0] = before
            else:
                net[0] = net[0] + sum(down[1:], down[0])
            for k in range(levels):
                ab = absorb[ct, k : k + 1, :]
                em = emit[ct, k : k + 1, :]
                acc = None
                for p in range(group):
                    t = jnp.exp2(kabs_ref[k, gs[p] : gs[p] + 8, :] * ab)
                    trans[k, p] = t
                    s = planck[p] * em
                    down[p] = s + t * (down[p] - s)
                    acc = down[p] if acc is None else acc + down[p]
                net[k + 1] = acc if half == 0 else net[k + 1] + acc
            up = [0.3 * d for d in down]
            for k in range(levels - 1, -1, -1):
                em = emit[ct, k : k + 1, :]
                acc = None
                for p in range(group):
                    s = planck[p] * em
                    up[p] = s + trans[k, p] * (up[p] - s)
                    acc = up[p] if acc is None else acc + up[p]
                net[k + 1] = net[k + 1] - acc
            net[0] = net[0] - acc
        for k in range(levels):
            row = jnp.sum(net[k] - net[k + 1], axis=0, keepdims=True) * scale
            heat[ct, k : k + 1, :] = heat[ct, k : k + 1, :] + row
        return carry

    lax.fori_loop(0, chunks * lanes // width, column, 0)
    per = lanes // width
    for c in range(chunks):
        for j in range(per):
            out_ref[c * levels : (c + 1) * levels, j * width : (j + 1) * width] = heat[c * per + j].astype(BF16)


def laplace_row(centre, above, below, left, right):
    lanes = centre.shape[1]
    lane = lax.broadcasted_iota(jnp.int32, centre.shape, 1)
    west = jnp.where(lane == 0, left, pltpu.roll(centre, 1, 1))
    east = jnp.where(lane == lanes - 1, right, pltpu.roll(centre, lanes - 1, 1))
    return above + below + west + east - 4.0 * centre


def gather_kernel(levels, table_ref, parent_ref, temp_ref, humid_ref, up_ref, dn_ref, lf_ref, rt_ref, out_ref):
    rows, _, lanes = temp_ref.shape
    tiles = table_ref.shape[0]
    chunks = table_ref.shape[1] // levels
    lo_iota = lax.broadcasted_iota(jnp.int32, (lanes, lanes), 0)
    for r in range(rows):
        low = parent_ref[r : r + 1, :] % lanes
        high = jnp.broadcast_to(parent_ref[r : r + 1, :] // lanes, (levels, lanes))
        onehot = (lo_iota == low).astype(F32).astype(BF16)

        def owner(i, acc):
            span = 4
            got = jnp.dot(
                table_ref[pl.ds(i * span, span)].reshape(span * chunks * levels, lanes),
                onehot,
                preferred_element_type=F32,
            )
            for c in range(span * chunks):
                acc = jnp.where(high == i * span * chunks + c, got[c * levels : (c + 1) * levels], acc)
            return acc

        picked = lax.fori_loop(0, tiles // 4, owner, jnp.zeros((levels, lanes), F32))
        centre = temp_ref[r].astype(F32)
        above = (temp_ref[r - 1] if r > 0 else up_ref[0]).astype(F32)
        below = (temp_ref[r + 1] if r < rows - 1 else dn_ref[0]).astype(F32)
        lap = laplace_row(centre, above, below, lf_ref[:, r : r + 1], rt_ref[:, r : r + 1])
        first = (centre + 0.2 * lap).astype(BF16).astype(F32)
        heat_f = picked + 0.5 * humid_ref[r].astype(F32)
        out_ref[r] = (first + 0.5 * heat_f).astype(BF16)


def laplace_kernel(x_ref, up_ref, dn_ref, lf_ref, rt_ref, out_ref):
    rows = x_ref.shape[0]
    for r in range(rows):
        centre = x_ref[r].astype(F32)
        above = (x_ref[r - 1] if r > 0 else up_ref[0]).astype(F32)
        below = (x_ref[r + 1] if r < rows - 1 else dn_ref[0]).astype(F32)
        lap = laplace_row(centre, above, below, lf_ref[:, r : r + 1], rt_ref[:, r : r + 1])
        out_ref[r] = (centre + 0.2 * lap).astype(BF16)


def halos(x):
    g, t = lax.axis_size("grp"), lax.axis_size("tile")
    ahead = lambda n: [(i, (i + 1) % n) for i in range(n)]
    back = lambda n: [((i + 1) % n, i) for i in range(n)]
    up = lax.ppermute(x[-1:], "grp", ahead(g))
    dn = lax.ppermute(x[:1], "grp", back(g))
    lf = lax.ppermute(jnp.transpose(x[:, :, -1]), "tile", ahead(t)).astype(F32)
    rt = lax.ppermute(jnp.transpose(x[:, :, 0]), "tile", back(t)).astype(F32)
    return up, dn, lf, rt


def on_device(temp, humid, parent, kabs, planck, top_flux):
    levels, rows, lanes = temp.shape
    tiles = lax.axis_size("tile")
    owned = rows * lanes // 4
    chunks = owned // lanes
    feats = 2 * levels + 16
    gpts = kabs.shape[0]
    params = pltpu.CompilerParams(vmem_limit_bytes=VMEM_LIMIT)

    x = jnp.transpose(temp, (1, 0, 2))
    h = jnp.transpose(humid, (1, 0, 2))
    ones = jnp.ones((rows, 16, lanes), BF16)
    vals = jnp.concatenate([x, h, ones], 1)
    partial = pl.pallas_call(
        functools.partial(partial_kernel, chunks),
        out_shape=jax.ShapeDtypeStruct((tiles, chunks * feats, lanes), BF16),
        grid=(tiles,),
        in_specs=[
            pl.BlockSpec((rows, feats, lanes), lambda i: (0, 0, 0)),
            pl.BlockSpec((rows, lanes), lambda i: (0, 0)),
        ],
        out_specs=pl.BlockSpec((1, chunks * feats, lanes), lambda i: (i, 0, 0)),
        scratch_shapes=[
            pltpu.VMEM((lanes, rows * lanes), BF16),
            pltpu.VMEM((chunks * feats, rows * lanes), BF16),
        ],
        compiler_params=params,
    )(vals, parent)
    recv = lax.all_to_all(partial, "tile", split_axis=0, concat_axis=0, tiled=True)

    kb = jnp.broadcast_to(jnp.transpose(kabs)[:, :, None], (levels, gpts, 128))
    pb = jnp.broadcast_to(planck[:, None], (gpts, 128))
    tb = jnp.broadcast_to(top_flux[:, None], (gpts, 128))
    ctiles = owned // 128
    octets = gpts // 8
    group = octets // 2 if octets % 2 == 0 else octets
    table = pl.pallas_call(
        functools.partial(radiate_kernel, levels, feats),
        out_shape=jax.ShapeDtypeStruct((chunks * levels, lanes), BF16),
        in_specs=[VSPEC] * 4,
        out_specs=VSPEC,
        scratch_shapes=[
            pltpu.VMEM((chunks * feats, lanes), F32),
            pltpu.VMEM((ctiles, levels, 128), F32),
            pltpu.VMEM((ctiles, levels, 128), F32),
            pltpu.VMEM((levels, group, 8, 128), F32),
            pltpu.VMEM((levels + 1, 8, 128), F32),
            pltpu.VMEM((ctiles, levels, 128), F32),
        ],
        compiler_params=params,
    )(recv, kb, pb, tb)
    tables = lax.all_gather(table, "tile", axis=0)

    second = pl.pallas_call(
        functools.partial(gather_kernel, levels),
        out_shape=jax.ShapeDtypeStruct((rows, levels, lanes), BF16),
        in_specs=[VSPEC] * 8,
        out_specs=VSPEC,
        compiler_params=params,
    )(tables, parent, x, h, *halos(x))
    out = pl.pallas_call(
        laplace_kernel,
        out_shape=jax.ShapeDtypeStruct((rows, levels, lanes), BF16),
        in_specs=[VSPEC] * 5,
        out_specs=VSPEC,
        compiler_params=params,
    )(second, *halos(second))
    return jnp.transpose(out, (1, 0, 2))


def solution(mesh):
    return jax.shard_map(
        on_device,
        mesh=mesh,
        in_specs=(P(None, "grp", "tile"), P(None, "grp", "tile"), P("grp", "tile"), P(), P(), P()),
        out_specs=P(None, "grp", "tile"),
        check_vma=False,
    )
```

```python
import functools
import math

import jax
import jax.numpy as jnp
from jax import lax
from jax.experimental import pallas as pl
from jax.experimental.pallas import tpu as pltpu
from jax.sharding import PartitionSpec as P

F32 = jnp.float32
BF16 = jnp.bfloat16
VMEM_LIMIT = 60 * 1024 * 1024
VSPEC = pl.BlockSpec(memory_space=pltpu.VMEM)


def partial_kernel(chunks, offset_ref, temp_ref, humid_ref, parent_ref, out_ref, onehot, masked):
    rows, levels, lanes = temp_ref.shape
    step = pl.program_id(0)
    owner = 2 * step + offset_ref[0]
    data = 2 * levels * chunks
    row = lax.broadcasted_iota(jnp.int32, (16, lanes), 0)

    @pl.when(step == 0)
    def _():
        lo_iota = lax.broadcasted_iota(jnp.int32, (lanes, lanes), 0)
        for r in range(rows):
            low = parent_ref[r : r + 1, :] % lanes
            onehot[:, r * lanes : (r + 1) * lanes] = (lo_iota == low).astype(F32).astype(BF16)

    for r in range(rows):
        high = jnp.broadcast_to(parent_ref[r : r + 1, :] // lanes, (16, lanes))
        part = slice(r * lanes, (r + 1) * lanes)
        for c in range(chunks):
            mask = (high == owner * chunks + c).astype(F32).astype(BF16)
            for v in range(levels // 16):
                src = slice(v * 16, (v + 1) * 16)
                at = c * 2 * levels + v * 16
                masked[at : at + 16, part] = temp_ref[r, src, :] * mask
                masked[at + levels : at + levels + 16, part] = humid_ref[r, src, :] * mask
        masked[data : data + 16, part] = (high == owner * chunks + row // 2).astype(F32).astype(BF16)
    total = lax.dot_general(
        masked[...], onehot[...], (((1,), (1,)), ((), ())), preferred_element_type=F32
    )
    out_ref[0, :data, :] = total[:data].astype(out_ref.dtype)
    count = total[data:]
    high = jnp.floor(count * (1.0 / 32.0))
    out_ref[0, data:, :] = jnp.where(row % 2 == 0, high, count - 32.0 * high).astype(out_ref.dtype)


def radiate_kernel(levels, feats, recv_ref, kabs_in, planck_ref, top_ref, out_ref, kabs_ref, sums, absorb, emit, trans, net, heat):
    tiles = recv_ref.shape[0]
    lanes = recv_ref.shape[2]
    chunks = recv_ref.shape[1] // feats
    octets = kabs_in.shape[0] // 8
    group = octets // 2 if octets % 2 == 0 else octets
    width = 128
    data = chunks * feats
    for k in range(levels):
        kabs_ref[k] = jnp.broadcast_to(kabs_in[:, k : k + 1], kabs_ref.shape[1:])

    def add(i, carry):
        at = pl.ds(pl.multiple_of(i * 16, 16), 16)
        acc = recv_ref[0, at, :].astype(F32)
        for s in range(1, tiles):
            acc = acc + recv_ref[s, at, :].astype(F32)
        sums[at, :] = acc
        return carry

    lax.fori_loop(0, data // 16 + 1, add, 0)
    for c in range(chunks):
        base = c * feats
        cnt = sums[data + 2 * c : data + 2 * c + 1, :] * 32.0
        cnt = cnt + sums[data + 2 * c + 1 : data + 2 * c + 2, :]
        cnt = jnp.maximum(cnt, 1.0)
        for j in range(lanes // width):
            part = slice(j * width, (j + 1) * width)
            ct = c * (lanes // width) + j
            tc = sums[base : base + levels, part] / cnt[:, part]
            hc = sums[base + levels : base + 2 * levels, part] / cnt[:, part]
            emit[ct] = jnp.exp(0.25 * tc)
            absorb[ct] = jnp.exp(0.5 * hc) * (-math.log2(math.e))
            heat[ct] = -0.5 * hc

    scale = levels / (octets * 8)

    def column(ct, carry):
        for half in range(octets // group):
            gs = [(half * group + p) * 8 for p in range(group)]
            planck = [jnp.broadcast_to(planck_ref[g : g + 8, :], (8, width)) for g in gs]
            down = [jnp.broadcast_to(top_ref[g : g + 8, :], (8, width)) for g in gs]
            if half == 0:
                before = sum(down[1:], down[0])
                net[0] = before
            else:
                net[0] = net[0] + sum(down[1:], down[0])
            for k in range(levels):
                ab = absorb[ct, k : k + 1, :]
                em = emit[ct, k : k + 1, :]
                acc = None
                for p in range(group):
                    t = jnp.exp2(kabs_ref[k, gs[p] : gs[p] + 8, :] * ab)
                    trans[k, p] = t
                    s = planck[p] * em
                    down[p] = s + t * (down[p] - s)
                    acc = down[p] if acc is None else acc + down[p]
                net[k + 1] = acc if half == 0 else net[k + 1] + acc
            up = [0.3 * d for d in down]
            for k in range(levels - 1, -1, -1):
                em = emit[ct, k : k + 1, :]
                acc = None
                for p in range(group):
                    s = planck[p] * em
                    up[p] = s + trans[k, p] * (up[p] - s)
                    acc = up[p] if acc is None else acc + up[p]
                net[k + 1] = net[k + 1] - acc
            net[0] = net[0] - acc
        for k in range(levels):
            row = jnp.sum(net[k] - net[k + 1], axis=0, keepdims=True) * scale
            heat[ct, k : k + 1, :] = heat[ct, k : k + 1, :] + row
        return carry

    lax.fori_loop(0, chunks * lanes // width, column, 0)
    per = lanes // width
    for c in range(chunks):
        for j in range(per):
            out_ref[c * levels : (c + 1) * levels, j * width : (j + 1) * width] = heat[c * per + j].astype(BF16)


def laplace_row(centre, above, below, left, right):
    lanes = centre.shape[1]
    lane = lax.broadcasted_iota(jnp.int32, centre.shape, 1)
    west = jnp.where(lane == 0, left, pltpu.roll(centre, 1, 1))
    east = jnp.where(lane == lanes - 1, right, pltpu.roll(centre, lanes - 1, 1))
    return above + below + west + east - 4.0 * centre


def gather_kernel(levels, table_ref, parent_ref, temp_ref, humid_ref, up_ref, dn_ref, lf_ref, rt_ref, out_ref):
    rows, _, lanes = temp_ref.shape
    tiles = table_ref.shape[0]
    chunks = table_ref.shape[1] // levels
    lo_iota = lax.broadcasted_iota(jnp.int32, (lanes, lanes), 0)
    for r in range(rows):
        low = parent_ref[r : r + 1, :] % lanes
        high = jnp.broadcast_to(parent_ref[r : r + 1, :] // lanes, (levels, lanes))
        onehot = (lo_iota == low).astype(F32).astype(BF16)

        def owner(i, acc):
            span = 4
            got = jnp.dot(
                table_ref[pl.ds(i * span, span)].reshape(span * chunks * levels, lanes),
                onehot,
                preferred_element_type=F32,
            )
            for c in range(span * chunks):
                acc = jnp.where(high == i * span * chunks + c, got[c * levels : (c + 1) * levels], acc)
            return acc

        picked = lax.fori_loop(0, tiles // 4, owner, jnp.zeros((levels, lanes), F32))
        centre = temp_ref[r].astype(F32)
        above = (temp_ref[r - 1] if r > 0 else up_ref[0]).astype(F32)
        below = (temp_ref[r + 1] if r < rows - 1 else dn_ref[0]).astype(F32)
        lap = laplace_row(centre, above, below, lf_ref[:, r : r + 1], rt_ref[:, r : r + 1])
        first = (centre + 0.2 * lap).astype(BF16).astype(F32)
        heat_f = picked + 0.5 * humid_ref[r].astype(F32)
        out_ref[r] = (first + 0.5 * heat_f).astype(BF16)


def laplace_kernel(x_ref, up_ref, dn_ref, lf_ref, rt_ref, out_ref):
    rows = x_ref.shape[0]
    for r in range(rows):
        centre = x_ref[r].astype(F32)
        above = (x_ref[r - 1] if r > 0 else up_ref[0]).astype(F32)
        below = (x_ref[r + 1] if r < rows - 1 else dn_ref[0]).astype(F32)
        lap = laplace_row(centre, above, below, lf_ref[:, r : r + 1], rt_ref[:, r : r + 1])
        out_ref[r] = (centre + 0.2 * lap).astype(BF16)


def halos(x):
    g, t = lax.axis_size("grp"), lax.axis_size("tile")
    ahead = lambda n: [(i, (i + 1) % n) for i in range(n)]
    back = lambda n: [((i + 1) % n, i) for i in range(n)]
    up = lax.ppermute(x[-1:], "grp", ahead(g))
    dn = lax.ppermute(x[:1], "grp", back(g))
    lf = lax.ppermute(jnp.transpose(x[:, :, -1]), "tile", ahead(t)).astype(F32)
    rt = lax.ppermute(jnp.transpose(x[:, :, 0]), "tile", back(t)).astype(F32)
    return up, dn, lf, rt


def on_device(temp, humid, parent, kabs, planck, top_flux):
    levels, rows, lanes = temp.shape
    tiles = lax.axis_size("tile")
    owned = rows * lanes // 4
    chunks = owned // lanes
    feats = 2 * levels
    gpts = kabs.shape[0]
    params = pltpu.CompilerParams(vmem_limit_bytes=VMEM_LIMIT)

    x = jnp.transpose(temp, (1, 0, 2))
    h = jnp.transpose(humid, (1, 0, 2))
    size = chunks * feats + 16
    core = lax.rem(lax.axis_index("tile"), 2)
    half = tiles // 2

    def partial_sums(offset, dtype):
        return pl.pallas_call(
            functools.partial(partial_kernel, chunks),
            out_shape=jax.ShapeDtypeStruct((half, size, lanes), dtype),
            grid=(half,),
            in_specs=[
                pl.BlockSpec(memory_space=pltpu.SMEM),
                pl.BlockSpec((rows, levels, lanes), lambda i: (0, 0, 0)),
                pl.BlockSpec((rows, levels, lanes), lambda i: (0, 0, 0)),
                pl.BlockSpec((rows, lanes), lambda i: (0, 0)),
            ],
            out_specs=pl.BlockSpec((1, size, lanes), lambda i: (i, 0, 0)),
            scratch_shapes=[
                pltpu.VMEM((lanes, rows * lanes), BF16),
                pltpu.VMEM((size, rows * lanes), BF16),
            ],
            compiler_params=params,
            cost_estimate=pl.CostEstimate(
                flops=2 * half * size * rows * lanes * lanes,
                bytes_accessed=4 * half * size * lanes,
                transcendentals=0,
            ),
        )(offset.reshape(1).astype(jnp.int32), x, h, parent)

    theirs = partial_sums(1 - core, BF16)
    given = lax.ppermute(theirs, "tile", [(i, i ^ 1) for i in range(tiles)])
    mine = partial_sums(core, F32)
    partial = (mine + given.astype(F32)).astype(BF16)
    groups = [list(range(c, tiles, 2)) for c in range(2)]
    recv = lax.all_to_all(
        partial, "tile", split_axis=0, concat_axis=0, tiled=True, axis_index_groups=groups
    )

    ctiles = owned // 128
    octets = gpts // 8
    group = octets // 2 if octets % 2 == 0 else octets
    table = pl.pallas_call(
        functools.partial(radiate_kernel, levels, feats),
        out_shape=jax.ShapeDtypeStruct((chunks * levels, lanes), BF16),
        in_specs=[VSPEC] * 4,
        out_specs=VSPEC,
        scratch_shapes=[
            pltpu.VMEM((levels, gpts, 128), F32),
            pltpu.VMEM((size, lanes), F32),
            pltpu.VMEM((ctiles, levels, 128), F32),
            pltpu.VMEM((ctiles, levels, 128), F32),
            pltpu.VMEM((levels, group, 8, 128), F32),
            pltpu.VMEM((levels + 1, 8, 128), F32),
            pltpu.VMEM((ctiles, levels, 128), F32),
        ],
        compiler_params=params,
    )(recv, kabs, planck[:, None], top_flux[:, None])
    tables = lax.all_gather(table, "tile", axis=0)

    second = pl.pallas_call(
        functools.partial(gather_kernel, levels),
        out_shape=jax.ShapeDtypeStruct((rows, levels, lanes), BF16),
        in_specs=[VSPEC] * 8,
        out_specs=VSPEC,
        compiler_params=params,
    )(tables, parent, x, h, *halos(x))
    out = pl.pallas_call(
        laplace_kernel,
        out_shape=jax.ShapeDtypeStruct((rows, levels, lanes), BF16),
        in_specs=[VSPEC] * 5,
        out_specs=VSPEC,
        compiler_params=params,
    )(second, *halos(second))
    return jnp.transpose(out, (1, 0, 2))


def solution(mesh):
    return jax.shard_map(
        on_device,
        mesh=mesh,
        in_specs=(P(None, "grp", "tile"), P(None, "grp", "tile"), P("grp", "tile"), P(), P(), P()),
        out_specs=P(None, "grp", "tile"),
        check_vma=False,
    )
```
